32 devices in a mesh: seq: 8 (over y, x, core), head: 4 (over z).
Axes of the slice: x: 2, y: 2, z: 4, core: 2. Of those that a mesh axis runs over, the one named last changes fastest.
Arguments:
- query: bfloat16 [1024, 96, 128], P(('seq', 'head')), may hold values from -15.6 to 15.6
- key_new: bfloat16 [1024, 8, 128], P('seq', 'head'), may hold values from -6 to 6
- value_new: bfloat16 [1024, 8, 128], P('seq', 'head'), may hold values from -6 to 6
- key_old: bfloat16 [1024, 8, 128], P('seq', 'head'), may hold values from -6 to 6
- value_old: bfloat16 [1024, 8, 128], P('seq', 'head'), may hold values from -6 to 6
- offset: int32 [1], replicated, may hold values from 0 to 1023
- windows: int32 [8], P('head'), may hold values from 512 to 1024, as said below
- grad_out: bfloat16 [1024, 96, 128], P(('seq', 'head')), may hold values from -6 to 6
Outputs:
- grad_query: float32 [1024, 96, 128], P(('seq', 'head'))
- grad_key_new: float32 [1024, 8, 128], P('seq', 'head')
- grad_value_new: float32 [1024, 8, 128], P('seq', 'head')
- grad_key_old: float32 [1024, 8, 128], P('seq', 'head')
- grad_value_old: float32 [1024, 8, 128], P('seq', 'head')
The draws below stay inside these ranges and needn't reach their ends.
Inputs may be any that keep to these rules, and one draw needn't show every extreme that they name: `windows`: one key-value head has a window of exactly 1024 tokens and another of exactly 512.
All inputs are finite; a program needn't handle non-finite values.
Results may differ from the reference program's by a relative error of at most 0.003.
Values may be sent and summed in bfloat16 or wider, within the bound.
A program may use at most 128 MiB of HBM per device.

```python
import math
import jax
import jax.numpy as jnp
from jax import lax

HQ = 96
KVH = 8
HD = 128
GROUP = 12
STRETCH = 1024


def draw_query(key, part):
    values = jax.random.truncated_normal(jax.random.fold_in(key, 23), -6.0, 6.0, (STRETCH, HQ, HD), jnp.float32)
    return values.astype(jnp.bfloat16)


def draw_key_new(key, part):
    values = jax.random.truncated_normal(jax.random.fold_in(key, 33), -6.0, 6.0, (STRETCH, KVH, HD), jnp.float32)
    return values.astype(jnp.bfloat16)


def draw_windows(key, part):
    picks = jax.random.randint(jax.random.fold_in(key, 41), (KVH,), STRETCH // 2, STRETCH + 1)
    order = jax.random.permutation(jax.random.fold_in(key, 42), KVH)
    places = jnp.arange(KVH)
    picks = jnp.where(places == order[0], STRETCH, picks)
    picks = jnp.where(places == order[1], STRETCH // 2, picks)
    return picks.astype(jnp.int32)


def shard_levels(rng, dims, split, least, top_value):
    gain, own = 1.0, jax.random.fold_in(rng, 6)
    for position, shards_of in split:
        heights = jnp.exp(jax.random.uniform(jax.random.fold_in(own, position), (shards_of,), jnp.float32, least / len(split), top_value / len(split)))
        gain = gain * jnp.repeat(heights, dims[position] // shards_of).reshape([-1 if axis == position else 1 for axis in range(len(dims))])
    return gain


def normal_values(key, extent, scale, most, pieces=(), held_as=jnp.bfloat16):
    values = jax.random.normal(key, extent, jnp.float32) * scale
    if len(pieces) > 0:
        values = shard_levels(key, extent, pieces, -0.22, 0.18) * values
    return jnp.clip(values, min=-most, max=most).astype(held_as)


def setup_inputs(seed: int = 0) -> dict:
    key_of = jax.random.split(jax.random.key(seed), 9)
    query = draw_query(jax.random.fold_in(key_of[8], 71), 0)
    key_new = draw_key_new(jax.random.fold_in(key_of[8], 71), 0)
    value_new = normal_values(key_of[2], (STRETCH, KVH, HD), 1.0, 6.0, ((0, 8), (1, 4)))
    key_old = normal_values(key_of[3], (STRETCH, KVH, HD), 1.0, 6.0, ((0, 8), (1, 4)))
    value_old = normal_values(key_of[4], (STRETCH, KVH, HD), 1.0, 6.0, ((0, 8), (1, 4)))
    offset = jax.random.randint(key_of[5], (1,), 0, STRETCH).astype(jnp.int32)
    windows = draw_windows(jax.random.fold_in(key_of[8], 71), 0)
    grad_out = normal_values(key_of[7], (STRETCH, HQ, HD), 1.0, 6.0, ((0, 32),))
    return {"query": query, "key_new": key_new, "value_new": value_new, "key_old": key_old, "value_old": value_old, "offset": offset, "windows": windows, "grad_out": grad_out}


def reference(query, key_new, value_new, key_old, value_old, offset, windows, grad_out):
    score_scale = 1.0 / math.sqrt(HD)
    slot_order = (jnp.arange(STRETCH, dtype=jnp.int32) + offset[0]) % STRETCH
    all_keys = jnp.concatenate([key_old[slot_order], key_new], axis=0)
    all_values = jnp.concatenate([value_old[slot_order], value_new], axis=0)
    row_block = math.gcd(STRETCH, 128)
    key_span = STRETCH + row_block
    block_starts = jnp.arange(STRETCH // row_block, dtype=jnp.int32) * row_block

    def visit_block(state_in, row_start):
        key_grads, value_grads = state_in
        queries = lax.dynamic_slice_in_dim(query, row_start, row_block, 0).astype(jnp.float32).reshape(row_block, KVH, GROUP, HD)
        out_grads = lax.dynamic_slice_in_dim(grad_out, row_start, row_block, 0).astype(jnp.float32).reshape(row_block, KVH, GROUP, HD)
        key_rows = lax.dynamic_slice_in_dim(all_keys, row_start, key_span, 0).astype(jnp.float32)
        value_rows = lax.dynamic_slice_in_dim(all_values, row_start, key_span, 0).astype(jnp.float32)
        query_pos = row_start + jnp.arange(row_block, dtype=jnp.int32)
        key_pos = row_start + jnp.arange(key_span, dtype=jnp.int32) - STRETCH
        key_row = key_pos[None, None, None, :]
        query_col = query_pos[:, None, None, None]
        seen = (key_row <= query_col) & (key_row > query_col - windows[None, :, None, None])
        scores = score_scale * jnp.einsum('qgjd,kgd->qgjk', queries, key_rows)
        masked = jnp.where(seen, scores, -jnp.inf)
        row_top = lax.optimization_barrier(jnp.max(masked, axis=-1, keepdims=True))
        log_total = row_top + jnp.log(lax.optimization_barrier(jnp.sum(jnp.exp(masked - row_top), axis=-1, keepdims=True)))
        weights = jnp.where(seen, jnp.exp(scores - log_total), 0.0)
        weight_grad = jnp.einsum('qgjd,kgd->qgjk', out_grads, value_rows)
        row_delta = lax.optimization_barrier(jnp.sum(weights * weight_grad, axis=-1, keepdims=True))
        dscore = lax.optimization_barrier((weights * (weight_grad - row_delta)).astype(jnp.bfloat16)).astype(jnp.float32)
        weights_low = lax.optimization_barrier(weights.astype(jnp.bfloat16)).astype(jnp.float32)
        query_grad = score_scale * jnp.einsum('qgjk,kgd->qgjd', dscore, key_rows)
        key_part = score_scale * jnp.einsum('qgjk,qgjd->kgd', dscore, queries)
        value_part = jnp.einsum('qgjk,qgjd->kgd', weights_low, out_grads)
        key_grads = lax.dynamic_update_slice_in_dim(key_grads, lax.dynamic_slice_in_dim(key_grads, row_start, key_span, 0) + key_part, row_start, 0)
        value_grads = lax.dynamic_update_slice_in_dim(value_grads, lax.dynamic_slice_in_dim(value_grads, row_start, key_span, 0) + value_part, row_start, 0)
        return ((key_grads, value_grads), query_grad.reshape(row_block, HQ, HD))
    zero_grads = jnp.zeros((2 * STRETCH, KVH, HD), jnp.float32)
    final_state, query_blocks = lax.scan(visit_block, (zero_grads, zero_grads), block_starts)
    key_grads, value_grads = final_state
    grad_query = query_blocks.reshape(STRETCH, HQ, HD)
    back_order = (jnp.arange(STRETCH, dtype=jnp.int32) - offset[0]) % STRETCH
    return (grad_query, key_grads[STRETCH:], value_grads[STRETCH:], key_grads[:STRETCH][back_order], value_grads[:STRETCH][back_order])
```

```python
import functools
import math

import jax
import jax.numpy as jnp
from jax import lax
from jax.experimental import pallas as pl
from jax.experimental.pallas import tpu as pltpu
from jax.sharding import PartitionSpec as P

NT = (((1,), (1,)), ((), ()))
NN = (((1,), (0,)), ((), ()))


def dot(a, b, dims):
    return lax.dot_general(a, b, dims, preferred_element_type=jnp.float32)


def band_kernel(
    heads, reach, win_ref, q_ref, do_ref, k_ref, kt_ref, v_ref, dq_ref, dk_ref, dv_ref, bias, dk_sum, dv_sum
):
    group, step = pl.program_id(0), pl.program_id(1)
    blocks, _, rows, width = q_ref.shape
    tokens = blocks * rows
    span = k_ref.shape[1]
    scale = 1.0 / math.sqrt(width)

    @pl.when(step == 0)
    def _():
        window = win_ref[group]
        place = lax.broadcasted_iota(jnp.int32, (span, tokens), 0) - reach
        token = lax.broadcasted_iota(jnp.int32, (span, tokens), 1)
        seen = (place <= token) & (place > token - window)
        bias[...] = jnp.where(seen, 0.0, -jnp.inf)

    q = jnp.concatenate([q_ref[:, h].reshape(tokens, width) for h in range(heads)], 0)
    do = jnp.concatenate([do_ref[:, h].reshape(tokens, width) for h in range(heads)], 0)
    keys, values = k_ref[0], v_ref[0]
    scores = dot(keys, q, NT) + jnp.concatenate([bias[...]] * heads, 1)
    top = jnp.max(scores, axis=0, keepdims=True)
    grown = jnp.exp2((scores - top) * (scale * math.log2(math.e)))
    total = jnp.sum(grown, axis=0, keepdims=True)
    weight_grad = dot(values, do, NT)
    inverse = 1.0 / total
    delta = jnp.sum(grown * weight_grad, axis=0, keepdims=True) * inverse
    weights = grown * inverse
    dscore = (weights * (weight_grad - delta)).astype(jnp.bfloat16)
    dk_part = dot(dscore, q, NN)
    dv_part = dot(weights.astype(jnp.bfloat16), do, NN)
    dqt = dot(kt_ref[0], dscore, NN) * scale
    for h in range(heads):
        piece = dqt[:, h * tokens : (h + 1) * tokens].T
        dq_ref[:, h] = piece.reshape(blocks, rows, width).astype(dq_ref.dtype)

    @pl.when(step == 0)
    def _():
        dk_sum[...] = dk_part
        dv_sum[...] = dv_part

    @pl.when(step > 0)
    def _():
        dk_sum[...] += dk_part
        dv_sum[...] += dv_part

    @pl.when(step == pl.num_programs(1) - 1)
    def _():
        dk_ref[0] = (dk_sum[...] * scale).astype(dk_ref.dtype)
        dv_ref[0] = dv_sum[...].astype(dv_ref.dtype)


def band(windows, q, do, k, kt, v, reach):
    blocks, all_heads, rows, width = q.shape
    groups, span, _ = k.shape
    tokens = blocks * rows
    per_group = all_heads // groups
    heads = max(
        h for h in (1, 2, 4) if per_group % h == 0 and (h <= 1 or h * tokens * span <= 700_000)
    )
    steps = per_group // heads
    row_spec = pl.BlockSpec((blocks, heads, rows, width), lambda g, s: (0, g * steps + s, 0, 0))
    key_spec = pl.BlockSpec((1, span, width), lambda g, s: (g, 0, 0))
    return pl.pallas_call(
        functools.partial(band_kernel, heads, reach),
        grid=(groups, steps),
        in_specs=[
            pl.BlockSpec(memory_space=pltpu.SMEM),
            row_spec,
            row_spec,
            key_spec,
            pl.BlockSpec((1, width, span), lambda g, s: (g, 0, 0)),
            key_spec,
        ],
        out_specs=[row_spec, key_spec, key_spec],
        out_shape=[
            jax.ShapeDtypeStruct(q.shape, jnp.bfloat16),
            jax.ShapeDtypeStruct(k.shape, jnp.bfloat16),
            jax.ShapeDtypeStruct(k.shape, jnp.bfloat16),
        ],
        scratch_shapes=[
            pltpu.VMEM((span, tokens), jnp.float32),
            pltpu.VMEM((span, width), jnp.float32),
            pltpu.VMEM((span, width), jnp.float32),
        ],
        compiler_params=pltpu.CompilerParams(vmem_limit_bytes=56 * 2**20),
    )(windows, q, do, k, kt, v)


def shards(query, key_new, value_new, key_old, value_old, offset, windows, grad_out):
    head_count = lax.axis_size("head")
    seq_count = lax.axis_size("seq")
    seq_rank = lax.axis_index("seq")
    rows, all_heads, width = query.shape
    tokens = rows * head_count
    total = tokens * seq_count
    groups = key_new.shape[1]
    span = total + tokens
    shift = offset[0]

    def to_heads(x):
        x = x.transpose(1, 0, 2).reshape(head_count, all_heads // head_count, rows, width)
        return lax.all_to_all(x, "head", split_axis=0, concat_axis=0, tiled=True)

    kv = jnp.stack([key_old, value_old, key_new, value_new]).transpose(0, 2, 1, 3)
    every = lax.all_gather(kv, "seq", axis=2, tiled=True)
    q, do = to_heads(query), to_heads(grad_out)
    old = jnp.concatenate([every[:2], every[:2]], axis=2)
    line = jnp.concatenate([lax.dynamic_slice_in_dim(old, shift, total, 2), every[2:]], axis=2)
    seen = lax.dynamic_slice_in_dim(line, seq_rank * tokens, span, 2)
    dq, dk, dv = band(windows, q, do, seen[0], seen[0].transpose(0, 2, 1), seen[1], total)
    dq = lax.all_to_all(dq, "head", split_axis=0, concat_axis=0, tiled=True)
    grad_query = dq.reshape(all_heads, rows, width).transpose(1, 0, 2).astype(jnp.float32)

    line = jnp.zeros((2, groups, 2 * total, width), jnp.bfloat16)
    line = lax.dynamic_update_slice_in_dim(line, jnp.stack([dk, dv]), seq_rank * tokens, 2)
    old = line[:, :, :total]
    old = lax.dynamic_slice_in_dim(
        jnp.concatenate([old, old], axis=2), lax.rem(total - shift, total), total, 2
    )
    terms = jnp.stack([old, line[:, :, total:]])
    terms = terms.reshape(4, groups, seq_count, tokens, width).transpose(2, 0, 1, 3, 4)
    terms = lax.all_to_all(terms, "seq", split_axis=0, concat_axis=0, tiled=True)
    grads = jnp.sum(terms.astype(jnp.float32), axis=0).transpose(0, 2, 1, 3)
    return (grad_query, grads[2], grads[3], grads[0], grads[1])


def solution(mesh):
    tokens = P(("seq", "head"), None, None)
    slots = P("seq", "head", None)
    return jax.shard_map(
        shards,
        mesh=mesh,
        in_specs=(tokens, slots, slots, slots, slots, P(), P("head"), tokens),
        out_specs=(tokens, slots, slots, slots, slots),
        check_vma=False,
    )
```

```python
import functools
import math

import jax
import jax.numpy as jnp
from jax import lax
from jax.experimental import pallas as pl
from jax.experimental.pallas import tpu as pltpu
from jax.sharding import PartitionSpec as P

MESH = pl.DeviceIdType.MESH
NT = (((1,), (1,)), ((), ()))
NN = (((1,), (0,)), ((), ()))


def dot(a, b, dims):
    return lax.dot_general(a, b, dims, preferred_element_type=jnp.float32)


def kernel(
    heads, seqs, per_group, heads_at_once,
    win_ref, off_ref, q_ref, do_ref, kv_ref,
    dq_ref, grad_ref,
    q_all, do_all, kv_all, line, keys_t, bias, sums, terms, term_out, term_in, dq_out, dq_in,
    q_send, q_recv, do_send, do_recv, kv_send, kv_recv, dq_send, dq_recv, old_send, old_recv, new_send, new_recv,
):
    hb = heads_at_once
    me_h, me_s = lax.axis_index("head"), lax.axis_index("seq")
    rows, width = q_ref.shape[2:]
    tokens = rows * heads
    groups = q_ref.shape[1] // per_group
    total = tokens * seqs
    span = total + tokens
    steps = per_group // hb
    chunks = groups * steps
    scale = 1.0 / math.sqrt(width)
    pair = 2 * width

    def peer_h(k):
        return lax.rem(me_h + k, heads)

    def peer_s(k):
        return lax.rem(me_s + k, seqs)

    def row_copy(src, dst, send, recv, chunk, there, slot):
        part = pl.ds(chunk * hb, hb)
        return pltpu.make_async_remote_copy(
            src_ref=src.at[there, part], dst_ref=dst.at[slot, part],
            send_sem=send.at[chunk, there], recv_sem=recv.at[chunk, slot],
            device_id={"head": there}, device_id_type=MESH,
        )

    def kv_copy(there, slot):
        return pltpu.make_async_remote_copy(
            src_ref=kv_ref, dst_ref=kv_all.at[slot],
            send_sem=kv_send.at[there], recv_sem=kv_recv.at[slot],
            device_id={"seq": there}, device_id_type=MESH,
        )

    def term_copy(group, kind, there, slot):
        send, recv = ((old_send, old_recv), (new_send, new_recv))[kind]
        return pltpu.make_async_remote_copy(
            src_ref=term_out.at[group, kind, there], dst_ref=term_in.at[group, kind, slot],
            send_sem=send.at[group, there], recv_sem=recv.at[group, slot],
            device_id={"seq": there}, device_id_type=MESH,
        )

    barrier = pltpu.get_barrier_semaphore()
    for k in range(1, heads):
        pl.semaphore_signal(barrier, inc=1, device_id={"head": peer_h(k)}, device_id_type=MESH)
    for k in range(1, seqs):
        pl.semaphore_signal(barrier, inc=1, device_id={"seq": peer_s(k)}, device_id_type=MESH)
    pl.semaphore_wait(barrier, heads + seqs - 2)

    @pl.loop(1, seqs)
    def _(k):
        kv_copy(peer_s(k), me_s).start()

    @pl.loop(0, chunks)
    def _(chunk):
        for k in range(1, heads):
            row_copy(q_ref, q_all, q_send, q_recv, chunk, peer_h(k), me_h).start()
            row_copy(do_ref, do_all, do_send, do_recv, chunk, peer_h(k), me_h).start()

    q_all[me_h] = q_ref[me_h]
    do_all[me_h] = do_ref[me_h]
    kv_all[me_s] = kv_ref[...]

    @pl.loop(1, seqs)
    def _(k):
        kv_copy(peer_s(k), peer_s(k)).wait_recv()

    base = lax.rem(off_ref[0] + me_s * tokens, total)
    old_rows = total - me_s * tokens

    def slot_of(row):
        slot = row + base
        return jnp.where(slot >= total, slot - total, slot)

    @pl.loop(0, seqs - me_s)
    def _(block):
        row = block * tokens + lax.broadcasted_iota(jnp.int32, (tokens, total), 0)
        slot = lax.broadcasted_iota(jnp.int32, (tokens, total), 1)
        pick = jnp.where(slot_of(row) == slot, 1.0, 0.0).astype(jnp.bfloat16)
        stored = kv_all[:, 0].reshape(total, groups * pair)
        line[pl.ds(block * tokens, tokens)] = dot(pick, stored, NN).astype(jnp.bfloat16)

    @pl.loop(0, me_s + 1)
    def _(block):
        line[pl.ds((seqs - me_s + block) * tokens, tokens)] = kv_all[block, 1]

    for group in range(groups):
        left = group * pair
        window = win_ref[group]
        place = lax.broadcasted_iota(jnp.int32, (span, tokens), 0) - total
        token = lax.broadcasted_iota(jnp.int32, (span, tokens), 1)
        bias[...] = jnp.where((place <= token) & (place > token - window), 0.0, -jnp.inf)
        keys_t[...] = line[:, left : left + width].T
        sums[...] = jnp.zeros_like(sums)

        @pl.loop(0, steps)
        def _(step):
            chunk = group * steps + step
            first = chunk * hb
            for k in range(1, heads):
                row_copy(q_ref, q_all, q_send, q_recv, chunk, peer_h(k), peer_h(k)).wait_recv()
                row_copy(do_ref, do_all, do_send, do_recv, chunk, peer_h(k), peer_h(k)).wait_recv()
            q = jnp.concatenate([q_all[:, first + h].reshape(tokens, width) for h in range(hb)], 0)
            do = jnp.concatenate([do_all[:, first + h].reshape(tokens, width) for h in range(hb)], 0)
            keys = line[:, left : left + width]
            values = line[:, left + width : left + pair]
            scores = dot(keys, q, NT) + jnp.concatenate([bias[...]] * hb, 1)
            top = jnp.max(scores, axis=0, keepdims=True)
            grown = jnp.exp2((scores - top) * (scale * math.log2(math.e)))
            inverse = 1.0 / jnp.sum(grown, axis=0, keepdims=True)
            weight_grad = dot(values, do, NT)
            delta = jnp.sum(grown * weight_grad, axis=0, keepdims=True) * inverse
            weights = grown * inverse
            dscore = (weights * (weight_grad - delta)).astype(jnp.bfloat16)
            dqt = dot(keys_t[...], dscore, NN) * scale
            for h in range(hb):
                piece = dqt[:, h * tokens : (h + 1) * tokens].T.astype(jnp.bfloat16)
                dq_out[:, first + h] = piece.reshape(heads, rows, width)
            for k in range(1, heads):
                row_copy(dq_out, dq_in, dq_send, dq_recv, chunk, peer_h(k), me_h).start()
            sums[:, :width] += dot(dscore, q, NN)
            sums[:, width:] += dot(weights.astype(jnp.bfloat16), do, NN)

        terms[:, :width] = (sums[:, :width] * scale).astype(jnp.bfloat16)
        terms[:, width:] = sums[:, width:].astype(jnp.bfloat16)

        @pl.loop(0, seqs)
        def _(k):
            there = peer_s(k)
            row = lax.broadcasted_iota(jnp.int32, (tokens, total), 1)
            slot = there * tokens + lax.broadcasted_iota(jnp.int32, (tokens, total), 0)
            chosen = (slot_of(row) == slot) & (row < old_rows)
            pick = jnp.where(chosen, 1.0, 0.0).astype(jnp.bfloat16)
            term_out[group, 0, there] = dot(pick, terms[:total], NN).astype(jnp.bfloat16)

            @pl.when(there <= me_s)
            def _():
                term_out[group, 1, there] = terms[pl.ds((seqs - me_s + there) * tokens, tokens)]

            @pl.when(k > 0)
            def _():
                term_copy(group, 0, there, me_s).start()

                @pl.when(there < me_s)
                def _():
                    term_copy(group, 1, there, me_s).start()

    for k in range(heads):
        there = peer_h(k)
        place = pl.ds(there * groups * per_group, groups * per_group)
        if k == 0:
            dq_ref[place] = dq_out[there].astype(jnp.float32)
            continue

        @pl.loop(0, chunks)
        def _(chunk):
            row_copy(dq_out, dq_in, dq_send, dq_recv, chunk, there, there).wait_recv()

        dq_ref[place] = dq_in[there].astype(jnp.float32)

    for group in range(groups):
        for kind in range(2):
            grad_ref[group, kind] = term_out[group, kind, me_s].astype(jnp.float32)

        @pl.loop(1, seqs)
        def _(k):
            there = peer_s(k)
            term_copy(group, 0, there, there).wait_recv()
            grad_ref[group, 0] += term_in[group, 0, there].astype(jnp.float32)

            @pl.when(there > me_s)
            def _():
                term_copy(group, 1, there, there).wait_recv()
                grad_ref[group, 1] += term_in[group, 1, there].astype(jnp.float32)

    @pl.loop(0, chunks)
    def _(chunk):
        for k in range(1, heads):
            row_copy(q_ref, q_all, q_send, q_recv, chunk, peer_h(k), me_h).wait_send()
            row_copy(do_ref, do_all, do_send, do_recv, chunk, peer_h(k), me_h).wait_send()
            row_copy(dq_out, dq_in, dq_send, dq_recv, chunk, peer_h(k), me_h).wait_send()

    @pl.loop(1, seqs)
    def _(k):
        there = peer_s(k)
        kv_copy(there, me_s).wait_send()
        for group in range(groups):
            term_copy(group, 0, there, me_s).wait_send()

            @pl.when(there < me_s)
            def _():
                term_copy(group, 1, there, me_s).wait_send()


def shards(query, key_new, value_new, key_old, value_old, offset, windows, grad_out):
    heads, seqs = lax.axis_size("head"), lax.axis_size("seq")
    rows, all_heads, width = query.shape
    tokens = rows * heads
    total = tokens * seqs
    groups = key_new.shape[1]
    span = total + tokens
    mine = all_heads // heads
    per_group = mine // groups
    hb = max(h for h in (1, 2, 4) if per_group % h == 0 and (h <= 1 or h * tokens * span <= 700_000))
    chunks = mine // hb

    def by_head(x):
        return x.transpose(1, 0, 2).reshape(heads, mine, rows, width)

    kv = jnp.stack([jnp.stack([key_old, value_old], 2), jnp.stack([key_new, value_new], 2)])
    kv = kv.reshape(2, tokens, groups * 2 * width)
    vmem = pl.BlockSpec(memory_space=pltpu.VMEM)
    smem = pl.BlockSpec(memory_space=pltpu.SMEM)
    narrow, wide = jnp.bfloat16, jnp.float32
    row_shape = (heads, mine, rows, width)
    row_sems = pltpu.SemaphoreType.DMA((chunks, heads))
    seq_sems = pltpu.SemaphoreType.DMA((seqs,))
    term_sems = pltpu.SemaphoreType.DMA((groups, seqs))
    term_shape = (groups, 2, seqs, tokens, 2 * width)
    dq, grads = pl.pallas_call(
        functools.partial(kernel, heads, seqs, per_group, hb),
        in_specs=[smem, smem, vmem, vmem, vmem],
        out_specs=[vmem, vmem],
        out_shape=[
            jax.ShapeDtypeStruct((all_heads, rows, width), wide),
            jax.ShapeDtypeStruct((groups, 2, tokens, 2 * width), wide),
        ],
        scratch_shapes=[
            pltpu.VMEM(row_shape, narrow),
            pltpu.VMEM(row_shape, narrow),
            pltpu.VMEM((seqs, 2, tokens, groups * 2 * width), narrow),
            pltpu.VMEM((span, groups * 2 * width), narrow),
            pltpu.VMEM((width, span), narrow),
            pltpu.VMEM((span, tokens), wide),
            pltpu.VMEM((span, 2 * width), wide),
            pltpu.VMEM((span, 2 * width), narrow),
            pltpu.VMEM(term_shape, narrow),
            pltpu.VMEM(term_shape, narrow),
            pltpu.VMEM(row_shape, narrow),
            pltpu.VMEM(row_shape, narrow),
            row_sems, row_sems, row_sems, row_sems, seq_sems, seq_sems,
            row_sems, row_sems, term_sems, term_sems, term_sems, term_sems,
        ],
        compiler_params=pltpu.CompilerParams(
            collective_id=0, has_side_effects=True, vmem_limit_bytes=62 * 2**20
        ),
    )(windows, offset, by_head(query), by_head(grad_out), kv)
    grad_query = dq.transpose(1, 0, 2)
    grads = grads.reshape(groups, 2, tokens, 2, width).transpose(1, 3, 2, 0, 4)
    return (grad_query, grads[1, 0], grads[1, 1], grads[0, 0], grads[0, 1])


def solution(mesh):
    tokens = P(("seq", "head"), None, None)
    slots = P("seq", "head", None)
    return jax.shard_map(
        shards,
        mesh=mesh,
        in_specs=(tokens, slots, slots, slots, slots, P(), P("head"), tokens),
        out_specs=(tokens, slots, slots, slots, slots),
        check_vma=False,
    )
```

```python
import functools
import math

import jax
import jax.numpy as jnp
from jax import lax
from jax.experimental import pallas as pl
from jax.experimental.pallas import tpu as pltpu
from jax.sharding import PartitionSpec as P

MESH = pl.DeviceIdType.MESH
NT = (((1,), (1,)), ((), ()))
NN = (((1,), (0,)), ((), ()))


def dot(a, b, dims):
    return lax.dot_general(a, b, dims, preferred_element_type=jnp.float32)


def kernel(
    heads, seqs, per_group, heads_at_once,
    win_ref, off_ref, q_ref, do_ref, ko_ref, vo_ref, kn_ref, vn_ref,
    dq_ref, grad_ref,
    q_all, do_all, kv_all, line, keys_t, bias, sums, terms, term_out, term_in, dq_out, dq_in,
    q_send, q_recv, do_send, do_recv, kv_send, kv_recv, pass_send, dq_send, dq_recv, old_send, old_recv, new_send, new_recv,
):
    hb = heads_at_once
    me_h, me_s = lax.axis_index("head"), lax.axis_index("seq")
    rows, width = q_ref.shape[2:]
    tokens = rows * heads
    groups = q_ref.shape[1] // per_group
    total = tokens * seqs
    span = total + tokens
    steps = per_group // hb
    chunks = groups * steps
    scale = 1.0 / math.sqrt(width)

    def peer_h(k):
        return lax.rem(me_h + k, heads)

    def peer_s(k):
        return lax.rem(me_s + k, seqs)

    def row_copy(src, dst, send, recv, chunk, there, slot):
        part = pl.ds(chunk * hb, hb)
        return pltpu.make_async_remote_copy(
            src_ref=src.at[there, part], dst_ref=dst.at[slot, part],
            send_sem=send.at[chunk, there], recv_sem=recv.at[chunk, slot],
            device_id={"head": there}, device_id_type=MESH,
        )

    def kv_copy(there, slot):
        return pltpu.make_async_remote_copy(
            src_ref=kv_all.at[me_s], dst_ref=kv_all.at[slot],
            send_sem=kv_send.at[there], recv_sem=kv_recv.at[slot],
            device_id={"seq": there}, device_id_type=MESH,
        )

    partner = me_s + 1 - 2 * lax.rem(me_s, 2)

    def pass_copy(slot):
        return pltpu.make_async_remote_copy(
            src_ref=kv_all.at[slot], dst_ref=kv_all.at[slot],
            send_sem=pass_send.at[slot], recv_sem=kv_recv.at[slot],
            device_id={"seq": partner}, device_id_type=MESH,
        )

    def term_copy(group, kind, there, slot):
        send, recv = ((old_send, old_recv), (new_send, new_recv))[kind]
        return pltpu.make_async_remote_copy(
            src_ref=term_out.at[group, kind, there], dst_ref=term_in.at[group, kind, slot],
            send_sem=send.at[group, there], recv_sem=recv.at[group, slot],
            device_id={"seq": there}, device_id_type=MESH,
        )

    for kind, ref in enumerate((ko_ref, vo_ref, kn_ref, vn_ref)):
        kv_all[me_s, kind] = ref[...]

    barrier = pltpu.get_barrier_semaphore()
    for k in range(1, heads):
        pl.semaphore_signal(barrier, inc=1, device_id={"head": peer_h(k)}, device_id_type=MESH)
    for k in range(1, seqs):
        pl.semaphore_signal(barrier, inc=1, device_id={"seq": peer_s(k)}, device_id_type=MESH)
    pl.semaphore_wait(barrier, heads + seqs - 2)

    @pl.loop(1, seqs // 2)
    def _(k):
        kv_copy(peer_s(2 * k), me_s).start()

    kv_copy(partner, me_s).start()

    @pl.loop(0, chunks)
    def _(chunk):
        for k in range(1, heads):
            row_copy(q_ref, q_all, q_send, q_recv, chunk, peer_h(k), me_h).start()
            row_copy(do_ref, do_all, do_send, do_recv, chunk, peer_h(k), me_h).start()

    q_all[me_h] = q_ref[me_h]
    do_all[me_h] = do_ref[me_h]

    @pl.loop(1, seqs // 2)
    def _(k):
        slot = peer_s(2 * k)
        kv_copy(slot, slot).wait_recv()
        pass_copy(slot).start()

    @pl.loop(0, seqs // 2)
    def _(k):
        slot = lax.rem(partner + 2 * k, seqs)
        kv_copy(slot, slot).wait_recv()

    base = lax.rem(off_ref[0] + me_s * tokens, total)
    old_rows = total - me_s * tokens

    def slot_of(row):
        slot = row + base
        return jnp.where(slot >= total, slot - total, slot)

    @pl.loop(0, seqs - me_s)
    def _(block):
        row = block * tokens + lax.broadcasted_iota(jnp.int32, (tokens, total), 0)
        slot = lax.broadcasted_iota(jnp.int32, (tokens, total), 1)
        pick = jnp.where(slot_of(row) == slot, 1.0, 0.0).astype(jnp.bfloat16)
        for kind in range(2):
            stored = kv_all[:, kind].reshape(total, groups * width)
            line[kind, pl.ds(block * tokens, tokens)] = dot(pick, stored, NN).astype(jnp.bfloat16)

    @pl.loop(0, me_s + 1)
    def _(block):
        for kind in range(2):
            line[kind, pl.ds((seqs - me_s + block) * tokens, tokens)] = kv_all[block, 2 + kind]

    for group in range(groups):
        left = group * width
        window = win_ref[group]
        place = lax.broadcasted_iota(jnp.int32, (span, tokens), 0) - total
        token = lax.broadcasted_iota(jnp.int32, (span, tokens), 1)
        bias[...] = jnp.where((place <= token) & (place > token - window), 0.0, -jnp.inf)
        keys_t[...] = line[0, :, left : left + width].T
        sums[...] = jnp.zeros_like(sums)

        @pl.loop(0, steps)
        def _(step):
            chunk = group * steps + step
            first = chunk * hb
            for k in range(1, heads):
                row_copy(q_ref, q_all, q_send, q_recv, chunk, peer_h(k), peer_h(k)).wait_recv()
                row_copy(do_ref, do_all, do_send, do_recv, chunk, peer_h(k), peer_h(k)).wait_recv()
            q = jnp.concatenate([q_all[:, first + h].reshape(tokens, width) for h in range(hb)], 0)
            do = jnp.concatenate([do_all[:, first + h].reshape(tokens, width) for h in range(hb)], 0)
            keys = line[0, :, left : left + width]
            values = line[1, :, left : left + width]
            scores = dot(keys, q, NT) + jnp.concatenate([bias[...]] * hb, 1)
            top = jnp.max(scores, axis=0, keepdims=True)
            grown = jnp.exp2((scores - top) * (scale * math.log2(math.e)))
            inverse = 1.0 / jnp.sum(grown, axis=0, keepdims=True)
            weight_grad = dot(values, do, NT)
            delta = jnp.sum(grown * weight_grad, axis=0, keepdims=True) * inverse
            weights = grown * inverse
            dscore = (weights * (weight_grad - delta)).astype(jnp.bfloat16)
            dqt = dot(keys_t[...], dscore, NN) * scale
            for h in range(hb):
                piece = dqt[:, h * tokens : (h + 1) * tokens].T.astype(jnp.bfloat16)
                dq_out[:, first + h] = piece.reshape(heads, rows, width)
            for k in range(1, heads):
                row_copy(dq_out, dq_in, dq_send, dq_recv, chunk, peer_h(k), me_h).start()
            sums[:, :width] += dot(dscore, q, NN)
            sums[:, width:] += dot(weights.astype(jnp.bfloat16), do, NN)

        terms[:, :width] = (sums[:, :width] * scale).astype(jnp.bfloat16)
        terms[:, width:] = sums[:, width:].astype(jnp.bfloat16)

        @pl.loop(0, seqs)
        def _(k):
            there = peer_s(k)
            row = lax.broadcasted_iota(jnp.int32, (tokens, total), 1)
            slot = there * tokens + lax.broadcasted_iota(jnp.int32, (tokens, total), 0)
            chosen = (slot_of(row) == slot) & (row < old_rows)
            pick = jnp.where(chosen, 1.0, 0.0).astype(jnp.bfloat16)
            term_out[group, 0, there] = dot(pick, terms[:total], NN).astype(jnp.bfloat16)

            @pl.when(there <= me_s)
            def _():
                term_out[group, 1, there] = terms[pl.ds((seqs - me_s + there) * tokens, tokens)]

            @pl.when(k > 0)
            def _():
                term_copy(group, 0, there, me_s).start()

                @pl.when(there < me_s)
                def _():
                    term_copy(group, 1, there, me_s).start()

    for k in range(heads):
        there = peer_h(k)
        place = pl.ds(there * groups * per_group, groups * per_group)
        if k == 0:
            dq_ref[place] = dq_out[there]
            continue

        @pl.loop(0, chunks)
        def _(chunk):
            row_copy(dq_out, dq_in, dq_send, dq_recv, chunk, there, there).wait_recv()

        dq_ref[place] = dq_in[there]

    for group in range(groups):
        for kind in range(2):
            grad_ref[group, kind] = term_out[group, kind, me_s].astype(jnp.float32)

        @pl.loop(1, seqs)
        def _(k):
            there = peer_s(k)
            term_copy(group, 0, there, there).wait_recv()
            grad_ref[group, 0] += term_in[group, 0, there].astype(jnp.float32)

            @pl.when(there > me_s)
            def _():
                term_copy(group, 1, there, there).wait_recv()
                grad_ref[group, 1] += term_in[group, 1, there].astype(jnp.float32)

    kv_copy(partner, me_s).wait_send()

    @pl.loop(1, seqs // 2)
    def _(k):
        kv_copy(peer_s(2 * k), me_s).wait_send()
        pass_copy(peer_s(2 * k)).wait_send()

    @pl.loop(0, chunks)
    def _(chunk):
        for k in range(1, heads):
            row_copy(q_ref, q_all, q_send, q_recv, chunk, peer_h(k), me_h).wait_send()
            row_copy(do_ref, do_all, do_send, do_recv, chunk, peer_h(k), me_h).wait_send()
            row_copy(dq_out, dq_in, dq_send, dq_recv, chunk, peer_h(k), me_h).wait_send()

    @pl.loop(1, seqs)
    def _(k):
        there = peer_s(k)
        for group in range(groups):
            term_copy(group, 0, there, me_s).wait_send()

            @pl.when(there < me_s)
            def _():
                term_copy(group, 1, there, me_s).wait_send()


def shards(query, key_new, value_new, key_old, value_old, offset, windows, grad_out):
    heads, seqs = lax.axis_size("head"), lax.axis_size("seq")
    rows, all_heads, width = query.shape
    tokens = rows * heads
    total = tokens * seqs
    groups = key_new.shape[1]
    span = total + tokens
    mine = all_heads // heads
    per_group = mine // groups
    hb = max(h for h in (1, 2, 4) if per_group % h == 0 and (h <= 1 or h * tokens * span <= 700_000))
    chunks = mine // hb

    def by_head(x):
        return x.transpose(1, 0, 2).reshape(heads, mine, rows, width)

    kv = [x.reshape(tokens, groups * width) for x in (key_old, value_old, key_new, value_new)]
    vmem = pl.BlockSpec(memory_space=pltpu.VMEM)
    smem = pl.BlockSpec(memory_space=pltpu.SMEM)
    narrow, wide = jnp.bfloat16, jnp.float32
    row_shape = (heads, mine, rows, width)
    row_sems = pltpu.SemaphoreType.DMA((chunks, heads))
    seq_sems = pltpu.SemaphoreType.DMA((seqs,))
    term_sems = pltpu.SemaphoreType.DMA((groups, seqs))
    term_shape = (groups, 2, seqs, tokens, 2 * width)
    dq, grads = pl.pallas_call(
        functools.partial(kernel, heads, seqs, per_group, hb),
        in_specs=[smem, smem] + [vmem] * 6,
        out_specs=[vmem, vmem],
        out_shape=[
            jax.ShapeDtypeStruct((all_heads, rows, width), narrow),
            jax.ShapeDtypeStruct((groups, 2, tokens, 2 * width), wide),
        ],
        scratch_shapes=[
            pltpu.VMEM(row_shape, narrow),
            pltpu.VMEM(row_shape, narrow),
            pltpu.VMEM((seqs, 4, tokens, groups * width), narrow),
            pltpu.VMEM((2, span, groups * width), narrow),
            pltpu.VMEM((width, span), narrow),
            pltpu.VMEM((span, tokens), wide),
            pltpu.VMEM((span, 2 * width), wide),
            pltpu.VMEM((span, 2 * width), narrow),
            pltpu.VMEM(term_shape, narrow),
            pltpu.VMEM(term_shape, narrow),
            pltpu.VMEM(row_shape, narrow),
            pltpu.VMEM(row_shape, narrow),
            row_sems, row_sems, row_sems, row_sems, seq_sems, seq_sems, seq_sems,
            row_sems, row_sems, term_sems, term_sems, term_sems, term_sems,
        ],
        compiler_params=pltpu.CompilerParams(
            collective_id=0, has_side_effects=True, vmem_limit_bytes=62 * 2**20
        ),
    )(windows, offset, by_head(query), by_head(grad_out), *kv)
    grad_query = lax.optimization_barrier(dq.transpose(1, 0, 2)).astype(wide)
    grads = grads.reshape(groups, 2, tokens, 2, width).transpose(1, 3, 2, 0, 4)
    return (grad_query, grads[1, 0], grads[1, 1], grads[0, 0], grads[0, 1])


def solution(mesh):
    tokens = P(("seq", "head"), None, None)
    slots = P("seq", "head", None)
    return jax.shard_map(
        shards,
        mesh=mesh,
        in_specs=(tokens, slots, slots, slots, slots, P(), P("head"), tokens),
        out_specs=(tokens, slots, slots, slots, slots),
        check_vma=False,
    )
```

```python
import functools
import math

import jax
import jax.numpy as jnp
from jax import lax
from jax.experimental import pallas as pl
from jax.experimental.pallas import tpu as pltpu
from jax.sharding import PartitionSpec as P

MESH = pl.DeviceIdType.MESH
NT = (((1,), (1,)), ((), ()))
NN = (((1,), (0,)), ((), ()))


def dot(a, b, dims):
    return lax.dot_general(a, b, dims, preferred_element_type=jnp.float32)


def kernel(
    heads, seqs, per_group, heads_at_once,
    win_ref, off_ref, q_ref, do_ref, ko_ref, vo_ref, kn_ref, vn_ref,
    dq_ref, gko_ref, gvo_ref, gkn_ref, gvn_ref,
    q_all, do_all, kv_all, line, grad_ref, keys_t, bias, sums, terms, term_out, term_in, dq_out, dq_in,
    q_send, q_recv, do_send, do_recv, kv_send, kv_recv, pass_send, dq_send, dq_recv, old_send, old_recv, new_send, new_recv,
):
    hb = heads_at_once
    me_h, me_s = lax.axis_index("head"), lax.axis_index("seq")
    rows, width = q_ref.shape[2:]
    tokens = rows * heads
    groups = q_ref.shape[1] // per_group
    total = tokens * seqs
    span = total + tokens
    steps = per_group // hb
    chunks = groups * steps
    scale = 1.0 / math.sqrt(width)

    def peer_h(k):
        return lax.rem(me_h + k, heads)

    def peer_s(k):
        return lax.rem(me_s + k, seqs)

    def row_copy(src, dst, send, recv, chunk, there, slot):
        part = pl.ds(chunk * hb, hb)
        return pltpu.make_async_remote_copy(
            src_ref=src.at[there, part], dst_ref=dst.at[slot, part],
            send_sem=send.at[chunk, there], recv_sem=recv.at[chunk, slot],
            device_id={"head": there}, device_id_type=MESH,
        )

    def kv_copy(there, slot):
        return pltpu.make_async_remote_copy(
            src_ref=kv_all.at[me_s], dst_ref=kv_all.at[slot],
            send_sem=kv_send.at[there], recv_sem=kv_recv.at[slot],
            device_id={"seq": there}, device_id_type=MESH,
        )

    partner = me_s + 1 - 2 * lax.rem(me_s, 2)

    def pass_copy(slot):
        return pltpu.make_async_remote_copy(
            src_ref=kv_all.at[slot], dst_ref=kv_all.at[slot],
            send_sem=pass_send.at[slot], recv_sem=kv_recv.at[slot],
            device_id={"seq": partner}, device_id_type=MESH,
        )

    def term_copy(group, kind, there, slot):
        send, recv = ((old_send, old_recv), (new_send, new_recv))[kind]
        return pltpu.make_async_remote_copy(
            src_ref=term_out.at[group, kind, there], dst_ref=term_in.at[group, kind, slot],
            send_sem=send.at[group, there], recv_sem=recv.at[group, slot],
            device_id={"seq": there}, device_id_type=MESH,
        )

    for kind, ref in enumerate((ko_ref, vo_ref, kn_ref, vn_ref)):
        kv_all[me_s, kind] = ref[...]

    barrier = pltpu.get_barrier_semaphore()
    for k in range(1, heads):
        pl.semaphore_signal(barrier, inc=1, device_id={"head": peer_h(k)}, device_id_type=MESH)
    for k in range(1, seqs):
        pl.semaphore_signal(barrier, inc=1, device_id={"seq": peer_s(k)}, device_id_type=MESH)
    pl.semaphore_wait(barrier, heads + seqs - 2)

    @pl.loop(1, seqs // 2)
    def _(k):
        kv_copy(peer_s(2 * k), me_s).start()

    kv_copy(partner, me_s).start()

    @pl.loop(0, chunks)
    def _(chunk):
        for k in range(1, heads):
            row_copy(q_ref, q_all, q_send, q_recv, chunk, peer_h(k), me_h).start()
            row_copy(do_ref, do_all, do_send, do_recv, chunk, peer_h(k), me_h).start()

    q_all[me_h] = q_ref[me_h]
    do_all[me_h] = do_ref[me_h]

    @pl.loop(1, seqs // 2)
    def _(k):
        slot = peer_s(2 * k)
        kv_copy(slot, slot).wait_recv()
        pass_copy(slot).start()

    @pl.loop(0, seqs // 2)
    def _(k):
        slot = lax.rem(partner + 2 * k, seqs)
        kv_copy(slot, slot).wait_recv()

    base = lax.rem(off_ref[0] + me_s * tokens, total)
    old_rows = total - me_s * tokens

    def slot_of(row):
        slot = row + base
        return jnp.where(slot >= total, slot - total, slot)

    @pl.loop(0, seqs - me_s)
    def _(block):
        row = block * tokens + lax.broadcasted_iota(jnp.int32, (tokens, total), 0)
        slot = lax.broadcasted_iota(jnp.int32, (tokens, total), 1)
        pick = jnp.where(slot_of(row) == slot, 1.0, 0.0).astype(jnp.bfloat16)
        for kind in range(2):
            stored = kv_all[:, kind].reshape(total, groups * width)
            line[kind, pl.ds(block * tokens, tokens)] = dot(pick, stored, NN).astype(jnp.bfloat16)

    @pl.loop(0, me_s + 1)
    def _(block):
        for kind in range(2):
            line[kind, pl.ds((seqs - me_s + block) * tokens, tokens)] = kv_all[block, 2 + kind]

    for group in range(groups):
        left = group * width
        window = win_ref[group]
        place = lax.broadcasted_iota(jnp.int32, (span, tokens), 0) - total
        token = lax.broadcasted_iota(jnp.int32, (span, tokens), 1)
        bias[...] = jnp.where((place <= token) & (place > token - window), 0.0, -jnp.inf)
        keys_t[...] = line[0, :, left : left + width].T
        sums[...] = jnp.zeros_like(sums)

        @pl.loop(0, steps)
        def _(step):
            chunk = group * steps + step
            first = chunk * hb
            for k in range(1, heads):
                row_copy(q_ref, q_all, q_send, q_recv, chunk, peer_h(k), peer_h(k)).wait_recv()
                row_copy(do_ref, do_all, do_send, do_recv, chunk, peer_h(k), peer_h(k)).wait_recv()
            q = jnp.concatenate([q_all[:, first + h].reshape(tokens, width) for h in range(hb)], 0)
            do = jnp.concatenate([do_all[:, first + h].reshape(tokens, width) for h in range(hb)], 0)
            keys = line[0, :, left : left + width]
            values = line[1, :, left : left + width]
            scores = dot(keys, q, NT) + jnp.concatenate([bias[...]] * hb, 1)
            top = jnp.max(scores, axis=0, keepdims=True)
            grown = jnp.exp2((scores - top) * (scale * math.log2(math.e)))
            inverse = 1.0 / jnp.sum(grown, axis=0, keepdims=True)
            weight_grad = dot(values, do, NT)
            delta = jnp.sum(grown * weight_grad, axis=0, keepdims=True) * inverse
            weights = grown * inverse
            dscore = (weights * (weight_grad - delta)).astype(jnp.bfloat16)
            dqt = dot(keys_t[...], dscore, NN) * scale
            for h in range(hb):
                piece = dqt[:, h * tokens : (h + 1) * tokens].T.astype(jnp.bfloat16)
                dq_out[:, first + h] = piece.reshape(heads, rows, width)
            for k in range(1, heads):
                row_copy(dq_out, dq_in, dq_send, dq_recv, chunk, peer_h(k), me_h).start()
            sums[:, :width] += dot(dscore, q, NN)
            sums[:, width:] += dot(weights.astype(jnp.bfloat16), do, NN)

        terms[:, :width] = (sums[:, :width] * scale).astype(jnp.bfloat16)
        terms[:, width:] = sums[:, width:].astype(jnp.bfloat16)

        @pl.loop(0, seqs)
        def _(k):
            there = peer_s(k)
            row = lax.broadcasted_iota(jnp.int32, (tokens, total), 1)
            slot = there * tokens + lax.broadcasted_iota(jnp.int32, (tokens, total), 0)
            chosen = (slot_of(row) == slot) & (row < old_rows)
            pick = jnp.where(chosen, 1.0, 0.0).astype(jnp.bfloat16)
            term_out[group, 0, there] = dot(pick, terms[:total], NN).astype(jnp.bfloat16)

            @pl.when(there <= me_s)
            def _():
                term_out[group, 1, there] = terms[pl.ds((seqs - me_s + there) * tokens, tokens)]

            @pl.when(k > 0)
            def _():
                term_copy(group, 0, there, me_s).start()

                @pl.when(there < me_s)
                def _():
                    term_copy(group, 1, there, me_s).start()

    for k in range(heads):
        there = peer_h(k)
        place = pl.ds(there * groups * per_group, groups * per_group)
        if k == 0:
            dq_ref[place] = dq_out[there]
            continue

        @pl.loop(0, chunks)
        def _(chunk):
            row_copy(dq_out, dq_in, dq_send, dq_recv, chunk, there, there).wait_recv()

        dq_ref[place] = dq_in[there]

    for group in range(groups):
        for kind in range(2):
            grad_ref[group, kind] = term_out[group, kind, me_s].astype(jnp.float32)

        @pl.loop(1, seqs)
        def _(k):
            there = peer_s(k)
            term_copy(group, 0, there, there).wait_recv()
            grad_ref[group, 0] += term_in[group, 0, there].astype(jnp.float32)

            @pl.when(there > me_s)
            def _():
                term_copy(group, 1, there, there).wait_recv()
                grad_ref[group, 1] += term_in[group, 1, there].astype(jnp.float32)

    for place, ref in enumerate((gko_ref, gvo_ref, gkn_ref, gvn_ref)):
        left = place % 2 * width
        for group in range(groups):
            ref[:, group] = grad_ref[group, place // 2, :, left : left + width]

    kv_copy(partner, me_s).wait_send()

    @pl.loop(1, seqs // 2)
    def _(k):
        kv_copy(peer_s(2 * k), me_s).wait_send()
        pass_copy(peer_s(2 * k)).wait_send()

    @pl.loop(0, chunks)
    def _(chunk):
        for k in range(1, heads):
            row_copy(q_ref, q_all, q_send, q_recv, chunk, peer_h(k), me_h).wait_send()
            row_copy(do_ref, do_all, do_send, do_recv, chunk, peer_h(k), me_h).wait_send()
            row_copy(dq_out, dq_in, dq_send, dq_recv, chunk, peer_h(k), me_h).wait_send()

    @pl.loop(1, seqs)
    def _(k):
        there = peer_s(k)
        for group in range(groups):
            term_copy(group, 0, there, me_s).wait_send()

            @pl.when(there < me_s)
            def _():
                term_copy(group, 1, there, me_s).wait_send()


def shards(query, key_new, value_new, key_old, value_old, offset, windows, grad_out):
    heads, seqs = lax.axis_size("head"), lax.axis_size("seq")
    rows, all_heads, width = query.shape
    tokens = rows * heads
    total = tokens * seqs
    groups = key_new.shape[1]
    span = total + tokens
    mine = all_heads // heads
    per_group = mine // groups
    hb = max(h for h in (1, 2, 4) if per_group % h == 0 and (h <= 1 or h * tokens * span <= 700_000))
    chunks = mine // hb

    def by_head(x):
        return x.transpose(1, 0, 2).reshape(heads, mine, rows, width)

    kv = [x.reshape(tokens, groups * width) for x in (key_old, value_old, key_new, value_new)]
    vmem = pl.BlockSpec(memory_space=pltpu.VMEM)
    smem = pl.BlockSpec(memory_space=pltpu.SMEM)
    narrow, wide = jnp.bfloat16, jnp.float32
    row_shape = (heads, mine, rows, width)
    row_sems = pltpu.SemaphoreType.DMA((chunks, heads))
    seq_sems = pltpu.SemaphoreType.DMA((seqs,))
    term_sems = pltpu.SemaphoreType.DMA((groups, seqs))
    term_shape = (groups, 2, seqs, tokens, 2 * width)
    dq, gko, gvo, gkn, gvn = pl.pallas_call(
        functools.partial(kernel, heads, seqs, per_group, hb),
        in_specs=[smem, smem] + [vmem] * 6,
        out_specs=[vmem] * 5,
        out_shape=[
            jax.ShapeDtypeStruct((all_heads, rows, width), narrow),
        ]
        + [jax.ShapeDtypeStruct(key_new.shape, wide)] * 4,
        scratch_shapes=[
            pltpu.VMEM(row_shape, narrow),
            pltpu.VMEM(row_shape, narrow),
            pltpu.VMEM((seqs, 4, tokens, groups * width), narrow),
            pltpu.VMEM((2, span, groups * width), narrow),
            pltpu.VMEM((groups, 2, tokens, 2 * width), wide),
            pltpu.VMEM((width, span), narrow),
            pltpu.VMEM((span, tokens), wide),
            pltpu.VMEM((span, 2 * width), wide),
            pltpu.VMEM((span, 2 * width), narrow),
            pltpu.VMEM(term_shape, narrow),
            pltpu.VMEM(term_shape, narrow),
            pltpu.VMEM(row_shape, narrow),
            pltpu.VMEM(row_shape, narrow),
            row_sems, row_sems, row_sems, row_sems, seq_sems, seq_sems, seq_sems,
            row_sems, row_sems, term_sems, term_sems, term_sems, term_sems,
        ],
        compiler_params=pltpu.CompilerParams(
            collective_id=0, has_side_effects=True, vmem_limit_bytes=62 * 2**20
        ),
    )(windows, offset, by_head(query), by_head(grad_out), *kv)
    grad_query = lax.optimization_barrier(dq.transpose(1, 0, 2)).astype(wide)
    return (grad_query, gkn, gvn, gko, gvo)


def solution(mesh):
    tokens = P(("seq", "head"), None, None)
    slots = P("seq", "head", None)
    return jax.shard_map(
        shards,
        mesh=mesh,
        in_specs=(tokens, slots, slots, slots, slots, P(), P("head"), tokens),
        out_specs=(tokens, slots, slots, slots, slots),
        check_vma=False,
    )
```
